32 devices in a mesh: fsdp: 32 (over z, y, x, core).
Axes of the slice: x: 2, y: 2, z: 4, core: 2. Of those that a mesh axis runs over, the one named last changes fastest.
Arguments:
- tokens: bfloat16 [16384, 768], P('fsdp'), may hold values from -6 to 6
- cotangent: bfloat16 [32, 1024, 768], P('fsdp'), may hold values from -6 to 6
- lengths: int32 [32], replicated, may hold values from 1 to 1024, 16384 in all
- deal_order: int32 [32], replicated, may hold values from 0 to 31, each once
- w_query: bfloat16 [768, 192], P('fsdp'), may hold values from -0.4375 to 0.4375
- w_key: bfloat16 [768, 192], P('fsdp'), may hold values from -0.4375 to 0.4375
- w_value: bfloat16 [768, 192], P('fsdp'), may hold values from -0.4375 to 0.4375
- b_query: bfloat16 [768], P('fsdp'), may hold values from -3 to 3
- b_value: bfloat16 [768], P('fsdp'), may hold values from -3 to 3
- w_dense: bfloat16 [768, 768], P('fsdp'), may hold values from -1.75 to 1.75
- b_dense: bfloat16 [768], P('fsdp'), may hold values from -3 to 3
- gain_attn: bfloat16 [768], P('fsdp'), may hold values from 0.25 to 1.75
- shift_attn: bfloat16 [768], P('fsdp'), may hold values from -3 to 3
- w_inner: bfloat16 [768, 768], P('fsdp'), may hold values from -0.4375 to 0.4375
- b_inner: bfloat16 [3072], P('fsdp'), may hold values from -3 to 3
- w_outer: bfloat16 [3072, 192], P('fsdp'), may hold values from -0.21875 to 0.21875
- b_outer: bfloat16 [768], P('fsdp'), may hold values from -3 to 3
- gain_ffn: bfloat16 [768], P('fsdp'), may hold values from 0.25 to 1.75
- shift_ffn: bfloat16 [768], P('fsdp'), may hold values from -3 to 3
Outputs:
- layer_out: bfloat16 [16384, 768], P('fsdp')
- input_grad: bfloat16 [16384, 768], P('fsdp')
- grad_w_query: float32 [768, 192], P('fsdp')
- grad_w_key: float32 [768, 192], P('fsdp')
- grad_w_value: float32 [768, 192], P('fsdp')
- grad_b_query: float32 [768], P('fsdp')
- grad_b_value: float32 [768], P('fsdp')
- grad_w_dense: float32 [768, 768], P('fsdp')
- grad_b_dense: float32 [768], P('fsdp')
- grad_gain_attn: float32 [768], P('fsdp')
- grad_shift_attn: float32 [768], P('fsdp')
- grad_w_inner: float32 [768, 768], P('fsdp')
- grad_b_inner: float32 [3072], P('fsdp')
- grad_w_outer: float32 [3072, 192], P('fsdp')
- grad_b_outer: float32 [768], P('fsdp')
- grad_gain_ffn: float32 [768], P('fsdp')
- grad_shift_ffn: float32 [768], P('fsdp')
The draws below stay inside these ranges and needn't reach their ends.
Inputs may be any that keep to these rules, and one draw needn't show every extreme that they name: The lengths sum to 16384; the longest is exactly 1024. `deal_order`: each sequence number appears once.
All inputs are finite; a program needn't handle non-finite values.
Results may differ from the reference program's by a relative error of at most 0.014.
The reference program's roundings to bfloat16 on the way count: a program that leaves them out, or rounds other values in their place, can miss the bound.
Values may be sent and summed in bfloat16 or wider, within the bound.
No kernel may reach another device: no remote copies, remote signals or barrier semaphores. Data moves between devices by JAX's collectives and lax.ppermute only.
A program may use at most 256 MiB of HBM per device.

```python
import math
import jax
import jax.numpy as jnp
import numpy as np
from jax import lax

D = 768
HEADS = 12
HDIM = 64
FF = 3072
GROUPS = 4
MAXLEN = 1024
SEQ_DEV = 1
DG = 192
FG = 768
TOKENS = 16384
SEQS = 32
N_FSDP = 32


def spiked(result, rng, source, target, shards_of, factor):
    owner, partner = [(jnp.arange(result.shape[position]) // (result.shape[position] // shards_of)).reshape([-1 if axis == position else 1 for axis in range(result.ndim)]) for position in (source, target)]
    chosen = jax.random.permutation(rng, shards_of)[partner]
    strong = (owner == chosen) | (owner == (partner + shards_of // 2) % shards_of)
    return jnp.where(strong, factor * result, result)


def block_levels(key, shape, cuts, smallest, top_value):
    factor_of = 1.0
    for position, shards_of in cuts:
        steps = jax.random.uniform(jax.random.fold_in(jax.random.fold_in(key, 6), position), (shards_of,), jnp.float32, smallest / len(cuts), top_value / len(cuts))
        factor_of = factor_of * jnp.repeat(jnp.exp(steps), shape[position] // shards_of).reshape((-1,) + (1,) * (len(shape) - 1 - position))
    return factor_of


def split_up(amount, total, limit, skew):
    loads = [(1 << 20) // math.isqrt(grade ** skew) + 1 for grade in range(2, amount + 1)]
    spare, given = total - limit - (amount - 1), [1] * (amount - 1)
    while spare > 0:
        candidates = [i for i in range(amount - 1) if given[i] < limit]
        mass, budget = sum([loads[i] for i in candidates]), spare
        for i in candidates:
            more = min(limit - given[i], max(1, budget * loads[i] // mass), spare)
            given[i] = given[i] + more
            spare = spare - more
    return np.array([limit] + given)


def uneven_parts(key, count, total, reach, skew):
    if count == 2:
        one = jax.random.randint(key, (), max(1, total - reach), min(reach, total - 1) + 1)
        return jnp.stack([one, total - one])
    sizes = jnp.asarray(split_up(count, total, reach, skew), jnp.int32)
    pairs = (count - 1) // 2
    giver, taker = sizes[1:1 + 2 * pairs:2], sizes[2:2 + 2 * pairs:2]
    margin = jnp.minimum(giver - 1, reach - taker)
    passed = jax.random.randint(jax.random.fold_in(key, 1), (pairs,), 0, 1 << 20) % (margin + 1)
    sizes = sizes.at[1:1 + 2 * pairs:2].set(giver - passed).at[2:2 + 2 * pairs:2].set(taker + passed)
    return sizes[jax.random.permutation(jax.random.fold_in(key, 2), count)]


def gaussian(stream_key, shape, width, most, split=(), kind=jnp.bfloat16):
    result = width * jax.random.normal(stream_key, shape, jnp.float32)
    if split:
        result = result * block_levels(stream_key, shape, split, -0.22, 0.18)
    return jnp.clip(result, -most, most).astype(kind)


def gaussian_with(key, dims, deviation, most, split, heavy, kind=jnp.bfloat16):
    result = deviation * jax.random.normal(key, dims, jnp.float32)
    if split:
        result = result * block_levels(key, dims, split, -0.22, 0.18)
    return jnp.clip(spiked(result, jax.random.fold_in(key, 3), *heavy), -most, most).astype(kind)


def setup_inputs(seed: int = 0) -> dict:
    key_of = jax.random.split(jax.random.key(seed), 20)
    tokens = gaussian(key_of[0], (TOKENS, D), 1.0, 6.0, ((0, 32),))
    cotangent = gaussian_with(key_of[1], (SEQS, MAXLEN, D), 1.0, 6.0, ((0, 32),), (0, 2, 32, 2.75))
    lengths = uneven_parts(key_of[2], SEQS, TOKENS, MAXLEN, 1).astype(jnp.int32)
    deal_order = jax.random.permutation(key_of[3], SEQS).astype(jnp.int32)
    w_query = gaussian(key_of[4], (D, DG), DG ** -0.5, 0.4375, ((0, 32),))
    w_key = gaussian(key_of[5], (D, DG), DG ** -0.5, 0.4375, ((0, 32),))
    w_value = gaussian(key_of[6], (D, DG), DG ** -0.5, 0.4375, ((0, 32),))
    b_query = gaussian(key_of[7], (D,), 0.5, 3.0, ((0, 32),))
    b_value = gaussian(key_of[8], (D,), 0.5, 3.0, ((0, 32),))
    w_dense = gaussian(key_of[9], (D, D), (D // 64) ** -0.5, 1.75, ((0, 32),))
    b_dense = gaussian(key_of[10], (D,), 0.5, 3.0, ((0, 32),))
    gain_attn = jnp.clip(1.0 + 0.15 * jax.random.normal(key_of[11], (D,), jnp.float32), 0.25, 1.75).astype(jnp.bfloat16)
    shift_attn = gaussian(key_of[12], (D,), 0.5, 3.0, ((0, 32),))
    w_inner = gaussian(key_of[13], (D, FG), DG ** -0.5, 0.4375, ((0, 32),))
    b_inner = gaussian(key_of[14], (FF,), 0.5, 3.0, ((0, 32),))
    w_outer = gaussian(key_of[15], (FF, DG), FG ** -0.5, 0.21875, ((0, 32),))
    b_outer = gaussian(key_of[16], (D,), 0.5, 3.0, ((0, 32),))
    gain_ffn = jnp.clip(1.0 + 0.15 * jax.random.normal(key_of[17], (D,), jnp.float32), 0.25, 1.75).astype(jnp.bfloat16)
    shift_ffn = gaussian(key_of[18], (D,), 0.5, 3.0, ((0, 32),))
    return {"tokens": tokens, "cotangent": cotangent, "lengths": lengths, "deal_order": deal_order, "w_query": w_query, "w_key": w_key, "w_value": w_value, "b_query": b_query, "b_value": b_value, "w_dense": w_dense, "b_dense": b_dense, "gain_attn": gain_attn, "shift_attn": shift_attn, "w_inner": w_inner, "b_inner": b_inner, "w_outer": w_outer, "b_outer": b_outer, "gain_ffn": gain_ffn, "shift_ffn": shift_ffn}


@jax.custom_vjp
def low(v):
    return lax.optimization_barrier(v.astype(jnp.bfloat16)).astype(jnp.float32)

@jax.custom_vjp
def low_back(v):
    return v

def low_keep(v):
    return (low(v), None)

def low_pass(kept, grad):
    return (grad,)

def back_keep(v):
    return (v, None)

def back_low(kept, grad):
    return (low(grad),)
low.defvjp(low_keep, low_pass)
low_back.defvjp(back_keep, back_low)
epsilon = 1e-06
score_scale = 0.125
masked_score = -1e+30
highest = lax.Precision.HIGHEST

def grouped(values, weight):
    leading = values.shape[:-1]
    parted = values.reshape(leading + (GROUPS, values.shape[-1] // GROUPS))
    blocks = weight.reshape(GROUPS, weight.shape[0] // GROUPS, weight.shape[1])
    joined = jnp.einsum('...gc,gco->...go', parted, blocks, precision=highest)
    return joined.reshape(leading + (GROUPS * weight.shape[1],))

def layer_norm(summed, norm_gain, norm_shift):
    row_mean = lax.optimization_barrier(jnp.mean(summed, axis=-1, keepdims=True))
    centred = summed - row_mean
    variance = lax.optimization_barrier(jnp.mean(centred * centred, axis=-1, keepdims=True))
    return centred * lax.rsqrt(variance + epsilon) * norm_gain + norm_shift

def slot_layer(slot_rows, slot_length, params):
    w_query, w_key, w_value, b_query, b_value, w_dense, b_dense, gain_attn, shift_attn, w_inner, b_inner, w_outer, b_outer, gain_ffn, shift_ffn = params
    slot_count = slot_rows.shape[0]
    head_shape = (slot_count, MAXLEN, HEADS, HDIM)
    query_heads = low(low_back(grouped(slot_rows, w_query)) + b_query).reshape(head_shape)
    key_heads = low(low_back(grouped(slot_rows, w_key))).reshape(head_shape)
    value_heads = low(low_back(grouped(slot_rows, w_value)) + b_value).reshape(head_shape)
    scores = jnp.einsum('bqhd,bkhd->bhqk', query_heads, key_heads, precision=highest) * score_scale
    key_valid = jnp.arange(MAXLEN, dtype=jnp.int32)[None, :] < slot_length[:, None]
    scores = low_back(jnp.where(key_valid[:, None, None, :], scores, masked_score))
    top_score = lax.optimization_barrier(jnp.max(scores, axis=-1, keepdims=True))
    lifted = jnp.exp(scores - top_score)
    softmaxed = lifted / lax.optimization_barrier(jnp.sum(lifted, axis=-1, keepdims=True))
    context = jnp.einsum('bhqk,bkhd->bqhd', low(softmaxed), value_heads, precision=highest)
    context = low(low_back(context.reshape(slot_count, MAXLEN, D)))
    attended = low_back(jnp.einsum('bld,de->ble', context, w_dense, precision=highest)) + b_dense
    hidden = layer_norm(slot_rows + attended, gain_attn, shift_attn)
    inner_pre = low_back(grouped(low(hidden), w_inner)) + b_inner
    active = low(jax.nn.gelu(inner_pre, approximate=False))
    outer = low_back(grouped(active, w_outer)) + b_outer
    return layer_norm(hidden + outer, gain_ffn, shift_ffn)

def reference(tokens, cotangent, lengths, deal_order, w_query, w_key, w_value, b_query, b_value, w_dense, b_dense, gain_attn, shift_attn, w_inner, b_inner, w_outer, b_outer, gain_ffn, shift_ffn):
    params = tuple((tensor.astype(jnp.float32) for tensor in (w_query, w_key, w_value, b_query, b_value, w_dense, b_dense, gain_attn, shift_attn, w_inner, b_inner, w_outer, b_outer, gain_ffn, shift_ffn)))
    starts = (jnp.cumsum(lengths) - lengths).astype(jnp.int32)
    seq_start = starts[deal_order]
    seq_length = lengths[deal_order]
    positions = jnp.arange(MAXLEN, dtype=jnp.int32)
    slot_valid = positions[None, :] < seq_length[:, None]
    slot_index_in = jnp.minimum(seq_start[:, None] + positions[None, :], TOKENS - 1).astype(jnp.int32)
    dealt = jnp.where(slot_valid[:, :, None], tokens.astype(jnp.float32)[slot_index_in], 0.0)

    def forward(dealt_in, weights):

        def one_group(carried, inputs):
            slot_rows, slot_length = inputs
            return (carried, slot_layer(slot_rows, slot_length, weights))
        unused, outputs = lax.scan(jax.checkpoint(one_group), jnp.zeros((), jnp.float32), (dealt_in.reshape(N_FSDP, SEQ_DEV, MAXLEN, D), seq_length.reshape(N_FSDP, SEQ_DEV)))
        return outputs.reshape(SEQS, MAXLEN, D)
    dealt_out, pullback = jax.vjp(forward, dealt, params)
    grad_dealt = jnp.where(slot_valid[:, :, None], cotangent.astype(jnp.float32), 0.0)
    grad_in, grad_params = pullback(grad_dealt)
    token_ids = jnp.arange(TOKENS, dtype=jnp.int32)
    seq_index = (jnp.searchsorted(starts, token_ids, side='right') - 1).astype(jnp.int32)
    inverse = jnp.zeros((SEQS,), jnp.int32).at[deal_order].set(jnp.arange(SEQS, dtype=jnp.int32))
    slot_index = (inverse[seq_index] * MAXLEN + token_ids - starts[seq_index]).astype(jnp.int32)
    layer_out = dealt_out.reshape(SEQS * MAXLEN, D)[slot_index].astype(jnp.bfloat16)
    input_grad = grad_in.reshape(SEQS * MAXLEN, D)[slot_index].astype(jnp.bfloat16)
    return (layer_out, input_grad, grad_params[0], grad_params[1], grad_params[2], grad_params[3], grad_params[4], grad_params[5], grad_params[6], grad_params[7], grad_params[8], grad_params[9], grad_params[10], grad_params[11], grad_params[12], grad_params[13], grad_params[14])
```

```python
from functools import partial

import jax
import jax.numpy as jnp
import numpy as np
from jax import lax
from jax.experimental import pallas as pl
from jax.experimental.pallas import tpu as pltpu
from jax.sharding import PartitionSpec as P

HEADS = 12
HDIM = 64
GROUPS = 4
HPG = HEADS // GROUPS
EPS = 1e-06
SCALE = 0.125
NEG = -1e30
LANE = 128
BLK = 256
WIN = 256
SLOTS = 5
PER = HPG * LANE
F32 = jnp.float32
BF16 = jnp.bfloat16
VMEM_LIMIT = 60 * 1024 * 1024


def dot(a, b):
    return lax.dot_general(a, b, (((1,), (0,)), ((), ())), preferred_element_type=F32)


def dot_nt(a, b):
    return lax.dot_general(a, b, (((1,), (1,)), ((), ())), preferred_element_type=F32)


def dot_tn(a, b):
    return lax.dot_general(a, b, (((0,), (0,)), ((), ())), preferred_element_type=F32)


def group_offset(g):
    return g * 192 // LANE * LANE


def lanes_of(shape):
    return lax.broadcasted_iota(jnp.int32, shape, len(shape) - 1)


def membership(base, seg_ref, rows):
    width = seg_ref.shape[1]
    position = base + lax.broadcasted_iota(jnp.int32, (rows, width), 0)
    return (position >= seg_ref[0:1, :]) & (position < seg_ref[1:2, :])


def tile3(value):
    return jnp.concatenate([value] * HPG, axis=1)


def table_list(tile):
    return 2 + 2 * SLOTS * tile


TABLE_BASE = 2 + 4 * SLOTS
TABLE_FLAG = TABLE_BASE + 2 * SLOTS
TABLE_CORE = TABLE_FLAG + SLOTS


def attn_fwd_kernel(
    seqs, lw, tbl, x0, x1, x2, x3, x4, raw, vec, seg, selc, selq, selo, spread_q, spread_v,
    kext, vext, qext, wq, wk, wv, ctx, lse, s_scr, m_scr, acc_scr, ctx_scr,
):
    g = pl.program_id(0)
    off = pl.multiple_of(group_offset(g), LANE)
    shift = pl.multiple_of(g * 192 - group_offset(g), HDIM)
    own = pl.ds(pl.multiple_of(g * 192, HDIM), 192)
    for i, (out, pick) in enumerate(((wq, spread_q), (wk, spread_q), (wv, spread_v))):
        out[...] = jnp.zeros_like(out)
        out[0, pl.ds(shift, 192), :] = dot(raw[own, i * WIN : (i + 1) * WIN], pick[...]).astype(BF16)
    bias_q = dot(vec[:, pl.ds(off, WIN)], selq[0])[0:1, :]
    lane_v = lanes_of((1, PER)) % LANE
    bias_v = dot(vec[:, pl.ds(off, WIN)], selo[0])[1:2, :]
    bias_v = jnp.where((lane_v >= HDIM) & (lane_v < HDIM + 3), 1.0, bias_v)
    xs = (x0, x1, x2, x3, x4)
    lane = lanes_of((BLK, lw))
    is_mask = (lane >= HDIM) & (lane < HDIM + seqs)
    is_lse = (lane >= HDIM + seqs) & (lane < HDIM + seqs + 3)
    plain = jnp.where(is_mask, NEG, jnp.where(is_lse, 1.0, 0.0)).astype(F32)
    for slot in range(SLOTS):

        @pl.when(tbl[TABLE_FLAG + slot] > 0)
        def _(slot=slot):
            for half in range(2):
                rows = pl.ds(half * BLK, BLK)
                chunk = 2 * slot + half
                into = pl.ds(chunk * BLK, BLK)
                member = membership(tbl[TABLE_BASE + chunk], seg, BLK)
                xc = xs[slot][rows, pl.ds(off, WIN)]
                kext[0, into, :] = (dot(xc, wk[0]) + tile3(jnp.where(member, 0.0, plain))).astype(BF16)
                vext[0, into, :] = (dot(xc, wv[0]) + bias_v).astype(BF16)
                if slot == 0:
                    qv = (dot(xc, wq[0]) + bias_q).astype(BF16).astype(F32) * SCALE
                    qext[0, rows, :] = (qv + tile3(jnp.where(member, 1.0, 0.0))).astype(BF16)

    @pl.when(g == 0)
    def _():
        lse[...] = jnp.zeros_like(lse)
        ctx_scr[...] = jnp.zeros_like(ctx_scr)

    for tile in range(2):
        count = tbl[tile]
        rows = pl.ds(tile * BLK, BLK)
        for h in range(HPG):
            m_scr[h] = jnp.full((BLK, LANE), -3e38, F32)
            acc_scr[h] = jnp.zeros((BLK, LANE), F32)

        def score_step(j, carry, tile=tile, rows=rows):
            start = pl.multiple_of(tbl[table_list(tile) + j] * BLK, BLK)
            for h in range(HPG):
                cols = pl.ds(h * lw, lw)
                s = dot_nt(qext[0, rows, cols], kext[0, pl.ds(start, BLK), cols])
                s_scr[h, :, pl.ds(pl.multiple_of(j * BLK, BLK), BLK)] = s
                m_scr[h] = jnp.maximum(m_scr[h], jnp.maximum(s[:, :LANE], s[:, LANE:]))
            return carry

        lax.fori_loop(0, count, score_step, 0)
        for h in range(HPG):
            m_scr[h] = jnp.broadcast_to(jnp.max(m_scr[h], axis=1, keepdims=True), (BLK, LANE))

        def value_step(j, carry, tile=tile):
            start = pl.multiple_of(tbl[table_list(tile) + j] * BLK, BLK)
            for h in range(HPG):
                top = m_scr[h]
                s = s_scr[h, :, pl.ds(pl.multiple_of(j * BLK, BLK), BLK)]
                p = jnp.exp(s - jnp.concatenate([top, top], axis=1)).astype(BF16)
                acc_scr[h] += dot(p, vext[0, pl.ds(start, BLK), pl.ds(h * LANE, LANE)])
            return carry

        lax.fori_loop(0, count, value_step, 0)
        lane_o = lanes_of((BLK, LANE))
        parts = []
        stat = lse[rows, :]
        for h in range(HPG):
            acc = acc_scr[h]
            total = acc[:, HDIM : HDIM + 1]
            parts.append(jnp.where(lane_o < HDIM, acc / total, 0.0).astype(BF16))
            minus = -(m_scr[h] + jnp.log(total))
            stat = jnp.where(lane_o == g * HPG + h, minus, stat)
        lse[rows, :] = stat
        packed = dot(jnp.concatenate(parts, axis=1), selc[0])
        ctx_scr[rows, pl.ds(off, WIN)] += packed

    @pl.when(g == GROUPS - 1)
    def _():
        ctx[...] = ctx_scr[...].astype(BF16)


def norm_stats(value):
    mean = jnp.mean(value, axis=1, keepdims=True)
    centred = value - mean
    root = lax.rsqrt(jnp.mean(centred * centred, axis=1, keepdims=True) + EPS)
    return centred * root, root


def norm_back(grad, normed, root, gain):
    q = grad * gain
    return root * (
        q
        - jnp.mean(q, axis=1, keepdims=True)
        - normed * jnp.mean(q * normed, axis=1, keepdims=True)
    )


def column_sum(value):
    return jnp.sum(value, axis=0, keepdims=True)


def mid_kernel(
    packed, core_ref, x, ctx, lse, cot, wd, wi_raw, wo_raw, vec_low, bi, widen, out, d_first, msg, *refs
):
    grads, refs = refs[: 2 if packed else 3], refs[2 if packed else 3 :]
    gvec, gbi, act_scr, slope_scr, row_scr, gwd_scr, gwi_scr, gwo_scr, wi, wo = refs
    step = pl.program_id(0)
    last = pl.num_programs(0) - 1

    @pl.when(step == 0)
    def _():
        gwd_scr[...] = jnp.zeros_like(gwd_scr)
        gwi_scr[...] = jnp.zeros_like(gwi_scr)
        gwo_scr[...] = jnp.zeros_like(gwo_scr)
        gvec[...] = jnp.zeros_like(gvec)
        gbi[...] = jnp.zeros_like(gbi)
        wi[...] = jnp.zeros_like(wi)
        for g in range(GROUPS):
            shift = g * 192 - group_offset(g)
            width = wi.shape[2]
            wi[g, shift : shift + 192, :] = wi_raw[g * 192 : (g + 1) * 192, :]
            wo[g] = dot(wo_raw[g * width : (g + 1) * width, :], widen[g % 2]).astype(BF16)

    vec = vec_low[...].astype(F32)
    b_dense, gain_a, shift_a = vec[2:3, :], vec[3:4, :], vec[4:5, :]
    b_outer, gain_f, shift_f = vec[5:6, :], vec[6:7, :], vec[7:8, :]
    first = x[...].astype(F32) + dot(ctx[...], wd[...]) + b_dense
    n1, r1 = norm_stats(first)
    hidden = n1 * gain_a + shift_a
    hidden_low = hidden.astype(BF16)
    ffg = wi.shape[2]
    row_scr[...] = hidden + b_outer
    for g in range(GROUPS):
        off = group_offset(g)
        cols = slice(g * ffg, (g + 1) * ffg)
        inner = dot(hidden_low[:, off : off + WIN], wi[g]) + bi[:, cols]
        half = 0.5 * (1.0 + lax.erf(inner * np.float32(np.sqrt(0.5))))
        act = (inner * half).astype(BF16)
        act_scr[:, cols] = act
        slope_scr[:, cols] = half + inner * jnp.exp(-0.5 * inner * inner) * np.float32(1.0 / np.sqrt(2.0 * np.pi))
        row_scr[:, off : off + WIN] += dot(act, wo[g])
    n2, r2 = norm_stats(row_scr[...])
    out[...] = (n2 * gain_f + shift_f).astype(BF16)
    grad = cot[...].astype(F32)
    gvec[4:5, :] += column_sum(grad * n2)
    gvec[5:6, :] += column_sum(grad)
    d_second = norm_back(grad, n2, r2, gain_f)
    gvec[3:4, :] += column_sum(d_second)
    d_outer_low = d_second.astype(BF16)
    row_scr[...] = d_second
    for g in range(GROUPS):
        off = group_offset(g)
        cols = slice(g * ffg, (g + 1) * ffg)
        d_low = d_outer_low[:, off : off + WIN]
        d_inner = dot_nt(d_low, wo[g]) * slope_scr[:, cols]
        gbi[:, cols] += column_sum(d_inner)
        d_inner_low = d_inner.astype(BF16)
        gwo_scr[g] += dot_tn(act_scr[:, cols], d_low)
        gwi_scr[g] += dot_tn(hidden_low[:, off : off + WIN], d_inner_low)
        row_scr[:, off : off + WIN] += dot_nt(d_inner_low, wi[g])
    d_hidden = row_scr[...]
    gvec[1:2, :] += column_sum(d_hidden * n1)
    gvec[2:3, :] += column_sum(d_hidden)
    d1 = norm_back(d_hidden, n1, r1, gain_a)
    gvec[0:1, :] += column_sum(d1)
    d_first[...] = d1
    d_low = d1.astype(BF16)
    gwd_scr[...] += dot_tn(ctx[...], d_low)
    d_ctx = dot_nt(d_low, wd[...]).astype(BF16)
    msg[:, : wd.shape[0]] = d_ctx
    prod = d_ctx.astype(F32) * ctx[...].astype(F32)
    rows = prod.shape[0]
    lane = lanes_of((rows, LANE))
    stat = lse[...]
    for t in range(HEADS // 2):
        pair = prod[:, t * LANE : (t + 1) * LANE]
        low = jnp.sum(jnp.where(lane < HDIM, pair, 0.0), axis=1, keepdims=True)
        high = jnp.sum(jnp.where(lane < HDIM, 0.0, pair), axis=1, keepdims=True)
        stat = jnp.where(lane == HEADS + 2 * t, -low, stat)
        stat = jnp.where(lane == HEADS + 2 * t + 1, -high, stat)
    hi = stat.astype(BF16).astype(F32)
    mid = (stat - hi).astype(BF16).astype(F32)
    low = (stat - hi - mid).astype(BF16).astype(F32)
    spread = hi + pltpu.roll(mid, 2 * HEADS, 1) + pltpu.roll(low, 4 * HEADS, 1)
    msg[:, wd.shape[0] :] = spread.astype(BF16)

    def write_plain():
        gwd, gwi, gwo = grads
        gwd[...] = gwd_scr[...].astype(BF16)
        for g in range(GROUPS):
            shift = g * 192 - group_offset(g)
            gwi[g * 192 : (g + 1) * 192, :] = gwi_scr[g, shift : shift + 192, :].astype(BF16)
            gwo[g * ffg : (g + 1) * ffg, :] = gwo_scr[g, :, shift : shift + 192].astype(BF16)

    def write_packed():
        keep, send = grads
        core = core_ref[0]
        chips, part = keep.shape[0], keep.shape[2]
        per_group = chips // GROUPS
        for chip in range(chips):
            g = chip // per_group
            shift = g * 192 - group_offset(g)
            for into, offset in ((keep, core), (send, 1 - core)):
                row = part * (2 * chip + offset)
                into[chip, 0] = gwd_scr[pl.ds(row, part), :].astype(BF16)
                local = part * (2 * (chip - g * per_group) + offset)
                into[chip, 1] = gwi_scr[g, pl.ds(shift + local, part), :].astype(BF16)
                pieces = [
                    gwo_scr[g, pl.ds(4 * local + part * q, part), :][:, shift : shift + 192] for q in range(4)
                ]
                into[chip, 2] = jnp.concatenate(pieces, axis=1).astype(BF16)

    pl.when(step == last)(write_packed if packed else write_plain)


def expand_grad(msg_rows, off, selo, seld, channels):
    body = msg_rows[:, pl.ds(off, WIN)]
    aux = msg_rows[:, channels : channels + LANE]
    return (dot(body, selo) + dot(aux, seld)).astype(BF16)


def query_back_kernel(
    seqs, lw, tbl, qext, kext, vext, msg, selo, seld, sell,
    dqp, gbq, q_scr, do_scr, acc_scr,
):
    g = pl.program_id(0)
    off = pl.multiple_of(group_offset(g), LANE)
    channels = msg.shape[1] - LANE
    aux = msg[:, channels : channels + LANE]
    do_scr[...] = (dot(msg[:, pl.ds(off, WIN)], selo[0]) + dot(aux, seld[0])).astype(BF16)
    q_scr[...] = (qext[0].astype(F32) + dot(aux, sell[0])).astype(BF16)
    sums = jnp.zeros((1, HPG * lw), F32)
    lane = lanes_of((BLK, lw))
    for tile in range(2):
        rows = pl.ds(tile * BLK, BLK)
        for h in range(HPG):
            acc_scr[h] = jnp.zeros((BLK, lw), F32)

        def step(j, carry, tile=tile, rows=rows):
            start = pl.multiple_of(tbl[table_list(tile) + j] * BLK, BLK)
            for h in range(HPG):
                cols = pl.ds(h * lw, lw)
                vcols = pl.ds(h * LANE, LANE)
                keys = kext[0, pl.ds(start, BLK), cols]
                p = jnp.exp(dot_nt(q_scr[rows, cols], keys))
                dp = dot_nt(do_scr[rows, vcols], vext[0, pl.ds(start, BLK), vcols])
                acc_scr[h] += dot((p * dp).astype(BF16), keys)
            return carry

        lax.fori_loop(0, tbl[tile], step, 0)
        dq = jnp.concatenate(
            [jnp.where(lane < HDIM, acc_scr[h] * SCALE, 0.0) for h in range(HPG)], axis=1
        )
        sums += column_sum(dq)
        dqp[rows, :] = dq.astype(BF16)
    gbq[0] = sums


def key_back_kernel(
    packed, seqs, lw, tbl, x0, x1, x2, x3, x4, g0, g1, g2, g3, g4, wq, wk, wv, vec, seg,
    kext, vext, selq, selo, seld, sell, selw, selv, dqp, d_first, out, *refs
):
    outs, refs = refs[: 2 if packed else 1], refs[2 if packed else 1 :]
    gbv, q_scr, do_scr, acck_scr, accv_scr, dx_scr, dk_scr, dv_scr, w_scr = refs
    g = pl.program_id(0)
    off = pl.multiple_of(group_offset(g), LANE)
    bias_q = dot(vec[:, pl.ds(off, WIN)], selq[0])[0:1, :]
    xs, gs = (x0, x1, x2, x3, x4), (g0, g1, g2, g3, g4)
    channels = g0.shape[1] - LANE
    for slot in range(SLOTS):

        @pl.when(tbl[TABLE_FLAG + slot] > 0)
        def _(slot=slot):
            for half in range(2):
                rows = pl.ds(half * BLK, BLK)
                chunk = 2 * slot + half
                into = pl.ds(chunk * BLK, BLK)
                member = membership(tbl[TABLE_BASE + chunk], seg, BLK)
                qv = (dot(xs[slot][rows, pl.ds(off, WIN)], wq[0]) + bias_q).astype(BF16).astype(F32) * SCALE
                aux = gs[slot][rows, channels : channels + LANE]
                extra = tile3(jnp.where(member, 1.0, 0.0)) + dot(aux, sell[0])
                q_scr[into, :] = (qv + extra).astype(BF16)
                body = gs[slot][rows, pl.ds(off, WIN)]
                do_scr[into, :] = (dot(body, selo[0]) + dot(aux, seld[0])).astype(BF16)

    sums = jnp.zeros((1, PER), F32)
    lane_k, lane_v = lanes_of((BLK, lw)), lanes_of((BLK, LANE))
    for tile in range(2):
        rows = pl.ds(tile * BLK, BLK)
        for h in range(HPG):
            acck_scr[h] = jnp.zeros((BLK, lw), F32)
            accv_scr[h] = jnp.zeros((BLK, LANE), F32)

        def step(j, carry, tile=tile, rows=rows):
            start = pl.multiple_of(tbl[table_list(tile) + j] * BLK, BLK)
            for h in range(HPG):
                cols = pl.ds(h * lw, lw)
                vcols = pl.ds(h * LANE, LANE)
                queries = q_scr[pl.ds(start, BLK), cols]
                grads = do_scr[pl.ds(start, BLK), vcols]
                p = jnp.exp(dot_nt(kext[0, rows, cols], queries))
                accv_scr[h] += dot(p.astype(BF16), grads)
                dp = dot_nt(vext[0, rows, vcols], grads)
                acck_scr[h] += dot((p * dp).astype(BF16), queries)
            return carry

        lax.fori_loop(0, tbl[tile], step, 0)
        dk = jnp.concatenate([jnp.where(lane_k < HDIM, acck_scr[h], 0.0) for h in range(HPG)], axis=1)
        dv = jnp.concatenate([jnp.where(lane_v < HDIM, accv_scr[h], 0.0) for h in range(HPG)], axis=1)
        sums += column_sum(dv)
        dk_scr[rows, :] = dk.astype(BF16)
        dv_scr[rows, :] = dv.astype(BF16)
    gbv[0] = sums

    @pl.when(g == 0)
    def _():
        dx_scr[...] = d_first[...]

    grads = (dqp[...], dk_scr[...], dv_scr[...])
    picks = (selw, selw, selv)
    weights = (wq, wk, wv)
    xg = x0[:, pl.ds(off, WIN)]
    total = jnp.zeros((xg.shape[0], WIN), F32)
    shift = g * 192 - group_offset(g)
    core = tbl[TABLE_CORE]
    for i in range(3):
        total += dot_nt(grads[i], weights[i][0])
        gwide = dot_tn(xg, grads[i]).astype(BF16)
        w_scr[...] = dot(gwide, picks[i][...])
        if not packed:
            outs[0][i] = w_scr[pl.ds(pl.multiple_of(shift, HDIM), 192), :].astype(BF16)
            continue
        keep, send = outs
        part = keep.shape[2]
        for chip in range(keep.shape[0]):
            row = shift + 2 * chip * part
            keep[chip, i] = w_scr[pl.ds(row + part * core, part), :].astype(BF16)
            send[chip, i] = w_scr[pl.ds(row + part * (1 - core), part), :].astype(BF16)
    dx_scr[:, pl.ds(off, WIN)] += total

    @pl.when(g == GROUPS - 1)
    def _():
        out[...] = dx_scr[...].astype(BF16)


def whole(shape):
    return pl.BlockSpec(shape, lambda *a: (0,) * len(shape))


def grouped_block(shape):
    return pl.BlockSpec((1,) + tuple(shape), lambda g, *a: (g,) + (0,) * len(shape))


def parity_block(shape):
    return pl.BlockSpec((1,) + tuple(shape), lambda g, *a: (g % 2,) + (0,) * len(shape))


def params_of(limit=VMEM_LIMIT):
    return pltpu.CompilerParams(dimension_semantics=("arbitrary",), vmem_limit_bytes=limit)


def selectors(lw, seqs):
    selc = np.zeros((2, PER, WIN), np.float32)
    for parity in range(2):
        for h in range(HPG):
            for e in range(HDIM):
                selc[parity, h * LANE + e, parity * 64 + h * HDIM + e] = 1
    seld = np.zeros((GROUPS, LANE, PER), np.float32)
    sell = np.zeros((GROUPS, LANE, HPG * lw), np.float32)
    for g in range(GROUPS):
        for h in range(HPG):
            for p in range(3):
                sell[g, 2 * HEADS * p + g * HPG + h, h * lw + HDIM + seqs + p] = 1
                seld[g, 2 * HEADS * p + HEADS + g * HPG + h, h * LANE + HDIM + p] = 1
    selw = np.zeros((HPG * lw, HPG * HDIM), np.float32)
    selv = np.zeros((PER, HPG * HDIM), np.float32)
    for h in range(HPG):
        for e in range(HDIM):
            selw[h * lw + e, h * HDIM + e] = 1
            selv[h * LANE + e, h * HDIM + e] = 1
    selq = np.zeros((2, WIN, HPG * lw), np.float32)
    widen = np.zeros((2, 192, WIN), np.float32)
    for parity in range(2):
        for h in range(HPG):
            for e in range(HDIM):
                selq[parity, parity * 64 + h * HDIM + e, h * lw + e] = 1
        for c in range(192):
            widen[parity, c, parity * 64 + c] = 1
    selo = selc.transpose(0, 2, 1)
    return {
        key: jnp.asarray(value, BF16)
        for key, value in dict(
            selc=selc, selo=selo, selq=selq, seld=seld, sell=sell, selw=selw, selv=selv, widen=widen,
            spread_q=selq[0], spread_v=selo[0],
        ).items()
    }


def select_kernel(tbl, got, out):
    count, spread, channels = out.shape
    seqs = (tbl.shape[0] - 2 * count - 1) // 3

    def one_peer(d, carry):
        base = tbl[3 * seqs + 2 * count] + d * spread * count

        def one_sequence(s, rows):
            block = got[tbl[2 * seqs + s], lax.rem(d, 2)].astype(F32)
            place = base + lax.broadcasted_iota(jnp.int32, (spread, channels), 0)
            return jnp.where((place >= tbl[s]) & (place < tbl[seqs + s]), block, rows)

        first, last = tbl[3 * seqs + d], tbl[3 * seqs + count + d]
        rows = lax.fori_loop(first, last + 1, one_sequence, jnp.zeros((spread, channels), F32))
        out[d] = rows.astype(BF16)
        return carry

    lax.fori_loop(0, count, one_peer, 0)


def per_device(
    tokens, cotangent, lengths, deal_order, w_query, w_key, w_value, b_query, b_value, w_dense, b_dense,
    gain_attn, shift_attn, w_inner, b_inner, w_outer, b_outer, gain_ffn, shift_ffn,
):
    n = lax.axis_size("fsdp")
    me = lax.axis_index("fsdp")
    rows, channels = tokens.shape
    seq_dev, max_len = cotangent.shape[0], cotangent.shape[1]
    seqs = lengths.shape[0]
    spread = rows // n
    assert seq_dev == 1 and max_len == 2 * rows and rows == 2 * BLK
    lw = -(-(HDIM + seqs + 3) // LANE) * LANE
    starts = (jnp.cumsum(lengths) - lengths).astype(jnp.int32)
    ends = starts + lengths

    def shift_by(value, by):
        return lax.ppermute(value, "fsdp", [(i, i + by) for i in range(n) if 0 <= i + by < n])

    def partner(value):
        return lax.ppermute(value, "fsdp", [(i, i ^ 1) for i in range(n)])

    even = me % 2 == 0

    def halo(value):
        before = shift_by(value, 2)
        after = shift_by(value, -2)
        beside = partner(value)
        passed = partner(jnp.where(even, after, before))
        return (value, before, after, beside, passed)

    near = jnp.where(even, 1, -1)
    deltas = jnp.stack([0 * near, 0 * near - 2, 0 * near + 2, near, -near]).astype(jnp.int32)
    x_win = halo(tokens)

    tile_low = me * rows + BLK * jnp.arange(2, dtype=jnp.int32)
    tile_high = tile_low + (BLK - 1)
    seq_of = lambda row: jnp.sum((starts[None, :] <= row[:, None]).astype(jnp.int32), axis=1) - 1
    low_row = jnp.sum(jnp.where(jnp.arange(seqs)[None, :] == seq_of(tile_low)[:, None], starts[None, :], 0), axis=1)
    high_row = jnp.sum(jnp.where(jnp.arange(seqs)[None, :] == seq_of(tile_high)[:, None], ends[None, :], 0), axis=1)
    chunk_low = low_row // BLK
    chunk_count = (high_row - 1) // BLK - chunk_low + 1
    slot_of = jnp.where(
        even, jnp.array([1, 4, 0, 3, 2], jnp.int32), jnp.array([1, 3, 0, 4, 2], jnp.int32)
    )
    chunk_at = jnp.stack([2 * slot_of, 2 * slot_of + 1], axis=1).reshape(-1)
    place = jnp.clip(
        chunk_low[:, None] + jnp.arange(2 * SLOTS, dtype=jnp.int32)[None, :] - 2 * (me - 2), 0, 2 * SLOTS - 1
    )
    lists = jnp.sum(
        jnp.where(place[:, :, None] == jnp.arange(2 * SLOTS)[None, None, :], chunk_at[None, None, :], 0), axis=2
    )
    bases = (((me + deltas) * rows)[:, None] + BLK * jnp.arange(2, dtype=jnp.int32)[None, :]).reshape(-1)
    first_dev, last_dev = low_row[0] // rows, (high_row[1] - 1) // rows
    flags = ((me + deltas >= first_dev) & (me + deltas <= last_dev)).astype(jnp.int32)
    core = (me % 2).astype(jnp.int32)
    table = jnp.concatenate([chunk_count, lists.reshape(-1), bases, flags, core[None]]).astype(jnp.int32)
    seg = jnp.zeros((8, lw), jnp.int32).at[0, HDIM : HDIM + seqs].set(starts).at[1, HDIM : HDIM + seqs].set(ends)

    chips = n // 2
    same_core = [[2 * c + k for c in range(chips)] for k in range(2)]
    exchange = lambda value: lax.all_to_all(
        value, "fsdp", split_axis=0, concat_axis=0, tiled=True, axis_index_groups=same_core
    )

    def gather(value):
        mine = exchange(jnp.broadcast_to(value[None], (chips,) + value.shape))
        other = partner(mine)
        pair = jnp.stack([jnp.where(even, mine, other), jnp.where(even, other, mine)], axis=1)
        return pair.reshape((n * value.shape[0],) + value.shape[1:])

    part = w_query.shape[0]
    gap = jnp.zeros((part, WIN - 192), BF16)
    small = jnp.stack([b_query, b_value, b_dense, gain_attn, shift_attn, b_outer, gain_ffn, shift_ffn], axis=1)
    small = jnp.concatenate([small, b_inner.reshape(4, part).T], axis=1)
    small = jnp.pad(small, ((0, 0), (0, WIN - 192 - small.shape[1])))
    pack_a = gather(jnp.concatenate([w_query, gap, w_key, gap, w_value, small], axis=1))
    pack_b = gather(jnp.concatenate([w_dense, w_inner], axis=1))
    full_outer = gather(w_outer)
    vec = jnp.pad(pack_a[:, 3 * WIN - 64 : 3 * WIN - 56].T, ((0, 8), (0, 0)))
    bi = pack_a[:, 3 * WIN - 56 : 3 * WIN - 52].reshape(n, part, 4).transpose(0, 2, 1).reshape(1, -1).astype(F32)
    ff_group = w_inner.shape[1]
    sel = selectors(lw, seqs)

    my_start = jnp.sum(jnp.where(jnp.arange(seqs) == deal_order[me], starts, 0))
    turn = my_start % max_len
    doubled = jnp.concatenate([cotangent[0], cotangent[0]], axis=0)
    rolled = lax.dynamic_slice_in_dim(doubled, (max_len - turn) % max_len, max_len)
    sent = rolled.reshape(2, n, spread, channels).transpose(1, 0, 2, 3)
    got = lax.all_to_all(sent, "fsdp", split_axis=0, concat_axis=0, tiled=True)
    ids = jnp.arange(seqs, dtype=jnp.int32)
    inverse = jnp.sum(jnp.where(deal_order[None, :] == ids[:, None], ids[None, :], 0), axis=1)
    block_low = rows * jnp.arange(n, dtype=jnp.int32) + spread * me
    route = jnp.concatenate(
        [starts, ends, inverse, seq_of(block_low), seq_of(block_low + spread - 1), (spread * me)[None]]
    ).astype(jnp.int32)
    passed = pl.pallas_call(
        select_kernel,
        out_shape=jax.ShapeDtypeStruct((n, spread, channels), BF16),
        grid_spec=pltpu.PrefetchScalarGridSpec(
            num_scalar_prefetch=1,
            grid=(1,),
            in_specs=[whole((n, 2, spread, channels))],
            out_specs=whole((n, spread, channels)),
        ),
        compiler_params=params_of(),
        name="route",
    )(route, got)
    cot = lax.all_to_all(passed, "fsdp", split_axis=0, concat_axis=0, tiled=True).reshape(rows, channels)

    win_rows = SLOTS * rows
    qw, vw = HPG * lw, PER
    sds = jax.ShapeDtypeStruct
    kext, vext, qext, wq_pad, wk_pad, wv_pad, ctx, lse = pl.pallas_call(
        partial(attn_fwd_kernel, seqs, lw),
        out_shape=(
            sds((GROUPS, win_rows, qw), BF16),
            sds((GROUPS, win_rows, vw), BF16),
            sds((GROUPS, rows, qw), BF16),
            sds((GROUPS, WIN, qw), BF16),
            sds((GROUPS, WIN, qw), BF16),
            sds((GROUPS, WIN, vw), BF16),
            sds((rows, channels), BF16),
            sds((rows, LANE), F32),
        ),
        grid_spec=pltpu.PrefetchScalarGridSpec(
            num_scalar_prefetch=1,
            grid=(GROUPS,),
            in_specs=[whole((rows, channels))] * SLOTS
            + [
                whole((channels, 3 * WIN)),
                whole((16, channels)),
                whole((8, lw)),
                parity_block((PER, WIN)),
                parity_block((WIN, qw)),
                parity_block((WIN, vw)),
                whole((WIN, qw)),
                whole((WIN, vw)),
            ],
            out_specs=[
                grouped_block((win_rows, qw)),
                grouped_block((win_rows, vw)),
                grouped_block((rows, qw)),
                grouped_block((WIN, qw)),
                grouped_block((WIN, qw)),
                grouped_block((WIN, vw)),
                whole((rows, channels)),
                whole((rows, LANE)),
            ],
            scratch_shapes=[
                pltpu.VMEM((HPG, BLK, win_rows), F32),
                pltpu.VMEM((HPG, BLK, LANE), F32),
                pltpu.VMEM((HPG, BLK, LANE), F32),
                pltpu.VMEM((rows, channels), F32),
            ],
        ),
        compiler_params=params_of(),
        name="attn_fwd",
    )(
        table, *x_win, pack_a, vec, seg, sel["selc"], sel["selq"], sel["selo"], sel["spread_q"], sel["spread_v"]
    )

    tile = BLK
    row_block = lambda width: pl.BlockSpec((tile, width), lambda i, *a: (i, 0))
    ff = GROUPS * ff_group
    packed = part % 8 == 0
    one_shapes = [(chips, 3, part, channels)] * 2
    if not packed:
        one_shapes = [(channels, channels), (channels, ff_group), (ff, 192)]
    layer_out, d_first, msg, *one, gvec, gbi = pl.pallas_call(
        partial(mid_kernel, packed),
        out_shape=(
            sds((rows, channels), BF16),
            sds((rows, channels), F32),
            sds((rows, channels + LANE), BF16),
            *[sds(shape, BF16) for shape in one_shapes],
            sds((8, channels), F32),
            sds((1, ff), F32),
        ),
        grid_spec=pltpu.PrefetchScalarGridSpec(
            num_scalar_prefetch=1,
            grid=(rows // tile,),
            in_specs=[
                row_block(channels),
                row_block(channels),
                row_block(LANE),
                row_block(channels),
                whole((channels, channels)),
                pl.BlockSpec((channels, ff_group), lambda i, *a: (0, 1)),
                whole((ff, 192)),
                whole((16, channels)),
                whole((1, ff)),
                whole((2, 192, WIN)),
            ],
            out_specs=[
                row_block(channels),
                row_block(channels),
                row_block(channels + LANE),
                *[whole(shape) for shape in one_shapes],
                whole((8, channels)),
                whole((1, ff)),
            ],
            scratch_shapes=[
                pltpu.VMEM((tile, ff), BF16),
                pltpu.VMEM((tile, ff), F32),
                pltpu.VMEM((tile, channels), F32),
                pltpu.VMEM((channels, channels), F32),
                pltpu.VMEM((GROUPS, WIN, ff_group), F32),
                pltpu.VMEM((GROUPS, ff_group, WIN), F32),
                pltpu.VMEM((GROUPS, WIN, ff_group), BF16),
                pltpu.VMEM((GROUPS, ff_group, WIN), BF16),
            ],
        ),
        compiler_params=params_of(),
        name="mid",
    )(core[None], tokens, ctx, lse, cot, pack_b, pack_b, full_outer, vec, bi, sel["widen"])

    def reduce_start(keep, send):
        both = keep.astype(F32) + partner(send).astype(F32)
        return exchange(both.astype(BF16))

    finish = lambda value: jnp.sum(value.astype(F32), axis=0)

    def split_cores(value):
        pairs = value.reshape((chips, 2) + value.shape[1:])
        return jnp.where(even, pairs[:, 0], pairs[:, 1]), jnp.where(even, pairs[:, 1], pairs[:, 0])

    if not packed:
        dense_g, inner_g = (value.reshape(n, part, channels) for value in one[:2])
        outer_g = one[2].reshape(n, 4, part, 192).transpose(0, 2, 1, 3).reshape(n, part, channels)
        one = split_cores(jnp.stack([dense_g, inner_g, outer_g], axis=1))
    sums_one = reduce_start(*one)
    msg_win = halo(msg)

    dqp, gbq = pl.pallas_call(
        partial(query_back_kernel, seqs, lw),
        out_shape=(sds((rows, GROUPS * qw), BF16), sds((GROUPS, 1, qw), F32)),
        grid_spec=pltpu.PrefetchScalarGridSpec(
            num_scalar_prefetch=1,
            grid=(GROUPS,),
            in_specs=[
                grouped_block((rows, qw)),
                grouped_block((win_rows, qw)),
                grouped_block((win_rows, vw)),
                whole((rows, channels + LANE)),
                parity_block((WIN, PER)),
                grouped_block((LANE, PER)),
                grouped_block((LANE, qw)),
            ],
            out_specs=[pl.BlockSpec((rows, qw), lambda g, *a: (0, g)), grouped_block((1, qw))],
            scratch_shapes=[
                pltpu.VMEM((rows, qw), BF16),
                pltpu.VMEM((rows, vw), BF16),
                pltpu.VMEM((HPG, BLK, lw), F32),
            ],
        ),
        compiler_params=params_of(),
        name="query_back",
    )(table, qext, kext, vext, msg, sel["selo"], sel["seld"], sel["sell"])

    two_block = pl.BlockSpec((chips // GROUPS, 3, part, 192), lambda g, *a: (g, 0, 0, 0))
    two_shapes, two_specs = [(chips, 3, part, 192)] * 2, [two_block] * 2
    if not packed:
        two_shapes, two_specs = [(3, channels, 192)], [pl.BlockSpec((3, 192, 192), lambda g, *a: (0, g, 0))]
    input_grad, *two, gbv = pl.pallas_call(
        partial(key_back_kernel, packed, seqs, lw),
        out_shape=(
            sds((rows, channels), BF16),
            *[sds(shape, BF16) for shape in two_shapes],
            sds((GROUPS, 1, vw), F32),
        ),
        grid_spec=pltpu.PrefetchScalarGridSpec(
            num_scalar_prefetch=1,
            grid=(GROUPS,),
            in_specs=[whole((rows, channels))] * SLOTS
            + [whole((rows, channels + LANE))] * SLOTS
            + [
                grouped_block((WIN, qw)),
                grouped_block((WIN, qw)),
                grouped_block((WIN, vw)),
                whole((16, channels)),
                whole((8, lw)),
                grouped_block((rows, qw)),
                grouped_block((rows, vw)),
                parity_block((WIN, qw)),
                parity_block((WIN, PER)),
                grouped_block((LANE, PER)),
                grouped_block((LANE, qw)),
                whole((qw, 192)),
                whole((vw, 192)),
                pl.BlockSpec((rows, qw), lambda g, *a: (0, g)),
                whole((rows, channels)),
            ],
            out_specs=[
                whole((rows, channels)),
                *two_specs,
                grouped_block((1, vw)),
            ],
            scratch_shapes=[
                pltpu.VMEM((win_rows, qw), BF16),
                pltpu.VMEM((win_rows, vw), BF16),
                pltpu.VMEM((HPG, BLK, lw), F32),
                pltpu.VMEM((HPG, BLK, LANE), F32),
                pltpu.VMEM((rows, channels), F32),
                pltpu.VMEM((rows, qw), BF16),
                pltpu.VMEM((rows, vw), BF16),
                pltpu.VMEM((WIN, 192), F32),
            ],
        ),
        compiler_params=params_of(),
        name="key_back",
    )(
        table, *x_win, *msg_win, wq_pad, wk_pad, wv_pad, vec, seg, kext, vext,
        sel["selq"], sel["selo"], sel["seld"], sel["sell"], sel["selw"], sel["selv"], dqp, d_first,
    )

    if not packed:
        two = split_cores(two[0].reshape(3, n, part, 192).transpose(1, 0, 2, 3))
    sums_two = finish(reduce_start(*two))
    g_query, g_key, g_value = sums_two[0], sums_two[1], sums_two[2]
    total_one = finish(sums_one)
    g_dense, g_inner = total_one[0], total_one[1]
    g_outer = total_one[2].reshape(part, 4, 192).transpose(1, 0, 2).reshape(4 * part, 192)
    head_sum = lambda value, width: value.reshape(GROUPS, HPG, width)[:, :, :HDIM].reshape(-1)
    vectors = jnp.concatenate(
        [
            jnp.stack([head_sum(gbq, lw), head_sum(gbv, LANE)] + [gvec[i] for i in range(6)], axis=1),
            gbi.reshape(n, 4, part).transpose(0, 2, 1).reshape(-1, 4),
        ],
        axis=1,
    )
    vector = jnp.sum(
        lax.all_to_all(vectors.reshape(n, part, 12), "fsdp", split_axis=0, concat_axis=0, tiled=True), axis=0
    )
    g_b_query, g_b_value, g_b_dense, g_gain_a, g_shift_a, g_b_outer, g_gain_f, g_shift_f = (
        vector[:, i] for i in range(8)
    )
    g_b_inner = vector[:, 8:12].T.reshape(-1)
    return (
        layer_out, input_grad, g_query, g_key, g_value, g_b_query, g_b_value, g_dense, g_b_dense,
        g_gain_a, g_shift_a, g_inner, g_b_inner, g_outer, g_b_outer, g_gain_f, g_shift_f,
    )


def solution(mesh):
    row, vec = P("fsdp", None), P("fsdp")
    in_specs = (
        row, P("fsdp", None, None), P(), P(), row, row, row, vec, vec, row, vec, vec, vec, row, vec, row, vec, vec, vec,
    )
    out_specs = (row, row, row, row, row, vec, vec, row, vec, vec, vec, row, vec, row, vec, vec, vec)
    return jax.shard_map(per_device, mesh=mesh, in_specs=in_specs, out_specs=out_specs, check_vma=False)
```
